32 devices in a mesh: ctx: 16 (over z, y, core), kvh: 2 (over x).
Axes of the slice: x: 2, y: 2, z: 4, core: 2. Of those that a mesh axis runs over, the one named last changes fastest.
Arguments:
- queries: bfloat16 [4096, 2048], P(('ctx', 'kvh')), may hold values from -6 to 6
- keys: bfloat16 [4096, 256], P(('ctx', 'kvh')), may hold values from -8 to 8
- values: bfloat16 [4096, 256], P(('ctx', 'kvh')), may hold values from -6 to 6
- grad_out: bfloat16 [4096, 2048], P(('ctx', 'kvh')), may hold values from -6 to 6
- doc_lengths: int32 [8], replicated, may hold values from 1 to 1024, 4096 in all
Outputs:
- attended: bfloat16 [4096, 2048], P(('ctx', 'kvh'))
- grad_queries: bfloat16 [4096, 2048], P(('ctx', 'kvh'))
- grad_keys: bfloat16 [4096, 256], P(('ctx', 'kvh'))
- grad_values: bfloat16 [4096, 256], P(('ctx', 'kvh'))
The draws below stay inside these ranges and needn't reach their ends.
Inputs may be any that keep to these rules, and one draw needn't show every extreme that they name: `doc_lengths`: 8 lengths that sum to 4096; the longest is exactly 1024.
All inputs are finite; a program needn't handle non-finite values.
Results may differ from the reference program's by a relative error of at most 0.0076.
Values may be sent and summed in bfloat16 or wider, within the bound.
A program may use at most 64 MiB of HBM per device.

```python
import math
import jax
import jax.numpy as jnp
import numpy as np
from jax import lax

HD = 128
QPG = 8
TD = 256
REACH = 4
KVH = 2
QH = 16
TOKENS = 4096
MAXDOC = 1024
DOCS = 8


def draw_queries(key, part):
    drawn = jax.random.normal(jax.random.fold_in(key, 1), (TOKENS, KVH, QPG, HD), jnp.float32)
    return jnp.clip(drawn, -6.0, 6.0).reshape(TOKENS, KVH * QPG * HD).astype(jnp.bfloat16)


def draw_keys(key, part):
    drawn = jax.random.normal(jax.random.fold_in(key, 2), (TOKENS, KVH, HD), jnp.float32)
    return jnp.clip(drawn, -8.0, 8.0).reshape(TOKENS, KVH * HD).astype(jnp.bfloat16)


def block_levels(key, shape, cuts, smallest, largest):
    factor_of = 1.0
    for axis_at, parts in cuts:
        heights = jax.random.uniform(jax.random.fold_in(jax.random.fold_in(key, 6), axis_at), (parts,), jnp.float32, smallest / len(cuts), largest / len(cuts))
        factor_of = factor_of * jnp.repeat(jnp.exp(heights), shape[axis_at] // parts).reshape((-1,) + (1,) * (len(shape) - 1 - axis_at))
    return factor_of


def profile(amount, total, bound, lean):
    portions = [(1 << 20) // math.isqrt(standing ** lean) + 1 for standing in range(2, amount + 1)]
    spare, given = total - bound - (amount - 1), [1] * (amount - 1)
    while spare > 0:
        free = [i for i in range(amount - 1) if given[i] < bound]
        pool, remaining = sum([portions[i] for i in free]), spare
        for i in free:
            extra = min(bound - given[i], max(1, remaining * portions[i] // pool), spare)
            given[i] = given[i] + extra
            spare = spare - extra
    return np.array([bound] + given)


def ragged_sizes(own_key, count, total, reach, skew):
    if count == 2:
        one = jax.random.randint(own_key, (), max(1, total - reach), min(reach, total - 1) + 1)
        return jnp.stack([one, total - one])
    sizes = jnp.asarray(profile(count, total, reach, skew), jnp.int32)
    couples = (count - 1) // 2
    giver, taker = sizes[1:1 + 2 * couples:2], sizes[2:2 + 2 * couples:2]
    margin = jnp.minimum(giver - 1, reach - taker)
    passed = jax.random.randint(jax.random.fold_in(own_key, 1), (couples,), 0, 1 << 20) % (margin + 1)
    sizes = sizes.at[1:1 + 2 * couples:2].set(giver - passed).at[2:2 + 2 * couples:2].set(taker + passed)
    return sizes[jax.random.permutation(jax.random.fold_in(own_key, 2), count)]


def gaussian(own_key, extent, spread, limit, shards=(), kind=jnp.bfloat16):
    entries = spread * jax.random.normal(own_key, extent, jnp.float32)
    if shards:
        entries = entries * block_levels(own_key, extent, shards, -0.22, 0.18)
    return jnp.clip(entries, -limit, limit).astype(kind)


def setup_inputs(seed: int = 0) -> dict:
    key_of = jax.random.split(jax.random.key(seed), 6)
    queries = draw_queries(jax.random.fold_in(key_of[5], 71), 0)
    keys = draw_keys(jax.random.fold_in(key_of[5], 71), 0)
    values = gaussian(key_of[2], (TOKENS, KVH * HD), 1.0, 6.0, ((0, 32),))
    grad_out = gaussian(key_of[3], (TOKENS, QH * HD), 1.0, 6.0, ((0, 32),))
    doc_lengths = ragged_sizes(key_of[4], DOCS, TOKENS, MAXDOC, 2).astype(jnp.int32)
    return {"queries": queries, "keys": keys, "values": values, "grad_out": grad_out, "doc_lengths": doc_lengths}


neg_large = -1e+30

def reference(queries, keys, values, grad_out, doc_lengths):
    lengths = doc_lengths.astype(jnp.int32)
    doc_ends = jnp.cumsum(lengths).astype(jnp.int32)
    starts = (doc_ends - lengths).astype(jnp.int32)
    scale_factor = 1.0 / math.sqrt(HD)
    offsets = jnp.arange(TD, dtype=jnp.int32)
    query_all = queries.reshape(TOKENS, KVH, QPG, HD)
    grad_all = grad_out.reshape(TOKENS, KVH, QPG, HD)
    zero_rows = jnp.zeros((MAXDOC, KVH, HD), jnp.bfloat16)
    key_all = jnp.concatenate([zero_rows, keys.reshape(TOKENS, KVH, HD)], 0)
    value_all = jnp.concatenate([zero_rows, values.reshape(TOKENS, KVH, HD)], 0)
    highest = lax.Precision.HIGHEST

    def first_of(positions):
        before_row = starts[None, :] <= positions[:, None]
        return lax.optimization_barrier(jnp.max(jnp.where(before_row, starts[None, :], 0), axis=1)).astype(jnp.int32)

    def block_inputs(block_index):
        first_row = (block_index * TD).astype(jnp.int32)
        query_block = lax.dynamic_slice_in_dim(query_all, first_row, TD, 0).astype(jnp.float32)
        grad_block = lax.dynamic_slice_in_dim(grad_all, first_row, TD, 0).astype(jnp.float32)
        query_pos = first_row + offsets
        return (first_row, query_block, grad_block, query_pos, first_of(query_pos))

    def tile_at(key_start, query_block, query_pos, doc_first):
        key_tile = lax.dynamic_slice_in_dim(key_all, key_start + MAXDOC, TD, 0).astype(jnp.float32)
        value_tile = lax.dynamic_slice_in_dim(value_all, key_start + MAXDOC, TD, 0).astype(jnp.float32)
        key_pos = key_start + offsets
        scores = jnp.einsum('qgpd,kgd->gpqk', query_block, key_tile, precision=highest) * scale_factor
        allowed = (key_pos[None, :] >= doc_first[:, None]) & (key_pos[None, :] <= query_pos[:, None])
        return (key_tile, value_tile, scores, allowed)

    def weights_of(scores, allowed, log_total):
        weights = jnp.where(allowed, jnp.exp(scores - log_total[..., None]), 0.0).astype(jnp.bfloat16)
        return lax.optimization_barrier(weights).astype(jnp.float32)

    def forward(block_index):
        first_row, query_block, grad_block, query_pos, doc_first = block_inputs(block_index)

        def gather_max(distance, loop_state):
            key_start = ((block_index - distance) * TD).astype(jnp.int32)

            def compute(partial_state):
                row_max, row_total = partial_state
                _, _, scores, allowed = tile_at(key_start, query_block, query_pos, doc_first)
                masked = jnp.where(allowed, scores, neg_large)
                new_max = jnp.maximum(row_max, masked.max(axis=3))
                row_total = row_total * jnp.exp(row_max - new_max) + lax.optimization_barrier(jnp.sum(jnp.where(allowed, jnp.exp(masked - new_max[..., None]), 0.0), axis=3))
                return (new_max, row_total)
            return lax.cond(doc_first[0] <= key_start + TD - 1, compute, lambda unchanged: unchanged, loop_state)
        start_state = (jnp.full((KVH, QPG, TD), neg_large, jnp.float32), jnp.zeros((KVH, QPG, TD), jnp.float32))
        row_max, row_total = lax.fori_loop(0, REACH + 1, gather_max, start_state)
        log_total = row_max + jnp.log(row_total)

        def add_out(distance, summed):
            key_start = ((block_index - distance) * TD).astype(jnp.int32)

            def compute(partial_state):
                _, value_tile, scores, allowed = tile_at(key_start, query_block, query_pos, doc_first)
                weights = weights_of(scores, allowed, log_total)
                return partial_state + jnp.einsum('gpqk,kgd->qgpd', weights, value_tile, precision=highest)
            return lax.cond(doc_first[0] <= key_start + TD - 1, compute, lambda unchanged: unchanged, summed)
        out_sum = lax.fori_loop(0, REACH + 1, add_out, jnp.zeros((TD, KVH, QPG, HD), jnp.float32))
        return (out_sum.astype(jnp.bfloat16), log_total)
    blocks = jnp.arange(TOKENS // TD, dtype=jnp.int32)
    attended_blocks, log_totals = lax.map(forward, blocks)
    attended = attended_blocks.reshape(TOKENS, QH * HD)
    kept_out = lax.optimization_barrier(attended)
    delta_all = lax.optimization_barrier(jnp.sum(grad_all.astype(jnp.float32) * kept_out.reshape(TOKENS, KVH, QPG, HD).astype(jnp.float32), axis=3))

    def backward(loop_state, inputs):
        block_index, log_total = inputs
        first_row, query_block, grad_block, query_pos, doc_first = block_inputs(block_index)
        delta_rows = jnp.transpose(lax.dynamic_slice_in_dim(delta_all, first_row, TD, 0), (1, 2, 0))

        def one_tile(distance, partial_state):
            key_start = ((block_index - distance) * TD).astype(jnp.int32)

            def compute(tile_state):
                grad_query, grad_key_sum, grad_value_sum = tile_state
                key_tile, value_tile, scores, allowed = tile_at(key_start, query_block, query_pos, doc_first)
                weights = weights_of(scores, allowed, log_total)
                grad_probs = jnp.einsum('qgpd,kgd->gpqk', grad_block, value_tile, precision=highest)
                grad_scores = (weights * (grad_probs - delta_rows[..., None]) * scale_factor).astype(jnp.bfloat16)
                grad_scores = lax.optimization_barrier(grad_scores).astype(jnp.float32)
                grad_query = grad_query + jnp.einsum('gpqk,kgd->qgpd', grad_scores, key_tile, precision=highest)
                key_part = jnp.einsum('gpqk,qgpd->kgd', grad_scores, query_block, precision=highest)
                value_part = jnp.einsum('gpqk,qgpd->kgd', weights, grad_block, precision=highest)
                row_at = key_start + MAXDOC
                grad_key_sum = lax.dynamic_update_slice_in_dim(grad_key_sum, lax.dynamic_slice_in_dim(grad_key_sum, row_at, TD, 0) + key_part, row_at, 0)
                grad_value_sum = lax.dynamic_update_slice_in_dim(grad_value_sum, lax.dynamic_slice_in_dim(grad_value_sum, row_at, TD, 0) + value_part, row_at, 0)
                return (grad_query, grad_key_sum, grad_value_sum)
            return lax.cond(doc_first[0] <= key_start + TD - 1, compute, lambda unchanged: unchanged, partial_state)
        start_query = jnp.zeros((TD, KVH, QPG, HD), jnp.float32)
        grad_query, grad_key_sum, grad_value_sum = lax.fori_loop(0, REACH + 1, one_tile, (start_query, loop_state[0], loop_state[1]))
        return ((grad_key_sum, grad_value_sum), grad_query.astype(jnp.bfloat16))
    zero_sums = jnp.zeros((TOKENS + MAXDOC, KVH, HD), jnp.float32)
    (grad_key_sum, grad_value_sum), grad_query_blocks = lax.scan(backward, (zero_sums, zero_sums), (blocks, log_totals))
    grad_queries = grad_query_blocks.reshape(TOKENS, QH * HD)
    grad_keys = grad_key_sum[MAXDOC:].astype(jnp.bfloat16).reshape(TOKENS, KVH * HD)
    grad_values = grad_value_sum[MAXDOC:].astype(jnp.bfloat16).reshape(TOKENS, KVH * HD)
    return (attended, grad_queries, grad_keys, grad_values)
```

```python
import functools
import math

import jax
import jax.numpy as jnp
from jax import lax
from jax.experimental import pallas as pl
from jax.experimental.pallas import tpu as pltpu
from jax.sharding import PartitionSpec as P

REACH = 4
LANES = 256
NEG_LARGE = -1e30
F32 = jnp.float32
BF16 = jnp.bfloat16


def matmul(a, b):
    return lax.dot_general(a, b, (((1,), (0,)), ((), ())), preferred_element_type=F32)


def kernel(
    ranges, groups, head_width, doc_ref, q_hbm, k_hbm, v_hbm, do_hbm,
    att_ref, gq_ref, gk_ref, gv_ref,
    q_ref, do_ref, kv_ref, kvt_ref, bias_ref, s_ref, e_ref, acc_ref, out_ref, in_ref,
    load_sem, kv_send, kv_recv, back_send, back_recv,
):
    tokens = q_ref.shape[0]
    reach = REACH * groups
    slots = reach + 1
    window = slots * tokens
    heads = q_ref.shape[1] // head_width // groups
    per_step = LANES // tokens
    steps = heads // per_step
    blocks = ranges * groups
    scale = 1.0 / math.sqrt(head_width)
    scale_2 = scale * math.log2(math.e)
    me = lax.axis_index("ctx") * groups + lax.axis_index("kvh")

    def device(block):
        return (block // groups, block % groups)

    def later(d):
        return pl.when(me + d < blocks)

    def earlier(d):
        return pl.when(me - d >= 0)

    def slot(s):
        return pl.ds(s * tokens, tokens)

    own_loads = []
    for g in range(groups):
        columns = pl.ds(g * head_width, head_width)
        for i, src in enumerate((k_hbm, v_hbm)):
            own_loads.append(
                pltpu.make_async_copy(
                    src.at[:, columns],
                    kv_ref.at[g, slot(reach), pl.ds(i * head_width, head_width)],
                    load_sem.at[2 * g + i],
                )
            )
    big_loads = [
        pltpu.make_async_copy(q_hbm, q_ref, load_sem.at[2 * groups]),
        pltpu.make_async_copy(do_hbm, do_ref, load_sem.at[2 * groups + 1]),
    ]
    for copy in own_loads + big_loads:
        copy.start()

    barrier = pltpu.get_barrier_semaphore()
    for d in range(1, reach + 1):

        @later(d)
        def _():
            pl.semaphore_signal(
                barrier, 1, device_id=device(me + d), device_id_type=pl.DeviceIdType.MESH
            )

        @earlier(d)
        def _():
            pl.semaphore_signal(
                barrier, 1, device_id=device(me - d), device_id_type=pl.DeviceIdType.MESH
            )

    def kv_copy(g, d):
        return pltpu.make_async_remote_copy(
            src_ref=kv_ref.at[g, slot(reach), :],
            dst_ref=kv_ref.at[g, slot(reach - d), :],
            send_sem=kv_send.at[g, d - 1],
            recv_sem=kv_recv.at[g, d - 1],
            device_id=device(me + d),
            device_id_type=pl.DeviceIdType.MESH,
        )

    def back_copy(g, d):
        return pltpu.make_async_remote_copy(
            src_ref=out_ref.at[g, slot(reach - d), :],
            dst_ref=in_ref.at[g, slot(d - 1), :],
            send_sem=back_send.at[g, d - 1],
            recv_sem=back_recv.at[g, d - 1],
            device_id=device(me - d),
            device_id_type=pl.DeviceIdType.MESH,
        )

    pl.semaphore_wait(barrier, jnp.minimum(me, reach) + jnp.minimum(blocks - 1 - me, reach))
    for copy in own_loads:
        copy.wait()
    for g in range(groups):
        for d in range(1, reach + 1):

            @later(d)
            def _():
                kv_copy(g, d).start()

    for d in range(1, reach + 1):

        @pl.when(me - d < 0)
        def _():
            for g in range(groups):
                kv_ref[g, slot(reach - d), :] = jnp.zeros((tokens, 2 * head_width), BF16)

    query_pos = me * tokens + lax.broadcasted_iota(jnp.int32, (8, LANES), 1) % tokens

    def next_doc(i, carry):
        start, first = carry
        first = jnp.where(start <= query_pos, jnp.maximum(first, start), first)
        return start + doc_ref[i], first

    _, doc_first = lax.fori_loop(
        0, doc_ref.shape[0], next_doc, (jnp.int32(0), jnp.zeros((8, LANES), jnp.int32))
    )
    for s in range(slots):
        key_pos = (me - reach + s) * tokens + lax.broadcasted_iota(jnp.int32, (tokens, LANES), 0)
        allowed = (key_pos >= doc_first[0:1]) & (key_pos <= query_pos[0:1])
        bias_ref[slot(s), :] = jnp.where(allowed, 0.0, NEG_LARGE)

    for copy in big_loads:
        copy.wait()

    for g in range(groups):
        for d in range(1, reach + 1):

            @earlier(d)
            def _():
                kv_copy(g, d).wait_recv()

        for s in range(slots):
            kvt_ref[:, slot(s)] = kv_ref[g, slot(s), :].T

        acc_ref[...] = jnp.zeros_like(acc_ref)

        def step(i, carry):
            first_head = g * heads + i * per_step

            def head_columns(j):
                return pl.ds(pl.multiple_of((first_head + j) * head_width, head_width), head_width)

            def stacked(ref):
                return jnp.concatenate([ref[:, head_columns(j)] for j in range(per_step)], axis=0)

            q = stacked(q_ref)
            do = stacked(do_ref)
            q_t = q.T
            do_t = do.T
            top = jnp.full((8, LANES), NEG_LARGE, F32)
            for s in range(slots):
                scores = matmul(kv_ref[g, slot(s), :head_width], q_t) * scale_2 + bias_ref[slot(s), :]
                s_ref[slot(s), :] = scores
                top = jnp.maximum(top, jnp.max(scores.reshape(tokens // 8, 8, LANES), axis=0))
            row_max = jnp.max(top, axis=0, keepdims=True)
            total = jnp.zeros((8, LANES), F32)
            for s in range(slots):
                weights = jnp.exp2(s_ref[slot(s), :] - row_max)
                total = total + jnp.sum(weights.reshape(tokens // 8, 8, LANES), axis=0)
                e_ref[slot(s), :] = weights.astype(BF16)
            inverse = 1.0 / jnp.sum(total, axis=0, keepdims=True)
            out_t = (matmul(kvt_ref[head_width:, :], e_ref[...]) * inverse).astype(BF16)
            delta = jnp.sum(out_t.astype(F32) * do_t.astype(F32), axis=0, keepdims=True)
            out = out_t.T
            scaled_do = (do_t.astype(F32) * inverse).astype(BF16).T
            gq_t = jnp.zeros((head_width, LANES), F32)
            for s in range(slots):
                weights = e_ref[slot(s), :]
                grad_probs = matmul(kv_ref[g, slot(s), head_width:], do_t)
                grad_scores = (weights.astype(F32) * ((grad_probs - delta) * inverse)).astype(BF16)
                gq_t = gq_t + matmul(kvt_ref[:head_width, slot(s)], grad_scores)
                acc_ref[slot(s), :head_width] += matmul(grad_scores, q)
                acc_ref[slot(s), head_width:] += matmul(weights, scaled_do)
            gq = (gq_t * scale).astype(BF16).T
            for j in range(per_step):
                att_ref[:, head_columns(j)] = out[j * tokens:(j + 1) * tokens]
                gq_ref[:, head_columns(j)] = gq[j * tokens:(j + 1) * tokens]
            return carry

        lax.fori_loop(0, steps, step, 0)

        for d in range(1, reach + 1):
            out_ref[g, slot(reach - d), :head_width] = (
                acc_ref[slot(reach - d), :head_width] * scale
            ).astype(BF16)
            out_ref[g, slot(reach - d), head_width:] = acc_ref[slot(reach - d), head_width:].astype(BF16)

            @earlier(d)
            def _():
                back_copy(g, d).start()

        columns = slice(g * head_width, (g + 1) * head_width)
        gk_ref[:, columns] = acc_ref[slot(reach), :head_width] * scale
        gv_ref[:, columns] = acc_ref[slot(reach), head_width:]

    for g in range(groups):
        columns = slice(g * head_width, (g + 1) * head_width)
        for d in range(1, reach + 1):

            @later(d)
            def _():
                back_copy(g, d).wait_recv()
                part = in_ref[g, slot(d - 1), :].astype(F32)
                gk_ref[:, columns] += part[:, :head_width]
                gv_ref[:, columns] += part[:, head_width:]

    for g in range(groups):
        for d in range(1, reach + 1):

            @later(d)
            def _():
                kv_copy(g, d).wait_send()

            @earlier(d)
            def _():
                back_copy(g, d).wait_send()


def on_device(ranges, groups, queries, keys, values, grad_out, doc_lengths):
    tokens = queries.shape[0]
    head_width = keys.shape[1] // groups
    reach = REACH * groups
    window = (reach + 1) * tokens
    anywhere = pl.BlockSpec(memory_space=pl.ANY)
    vmem = pl.BlockSpec(memory_space=pltpu.VMEM)
    dma = pltpu.SemaphoreType.DMA
    attended, grad_queries, grad_keys, grad_values = pl.pallas_call(
        functools.partial(kernel, ranges, groups, head_width),
        out_shape=(
            jax.ShapeDtypeStruct(queries.shape, BF16),
            jax.ShapeDtypeStruct(queries.shape, BF16),
            jax.ShapeDtypeStruct(keys.shape, F32),
            jax.ShapeDtypeStruct(keys.shape, F32),
        ),
        in_specs=[pl.BlockSpec(memory_space=pltpu.SMEM)] + [anywhere] * 4,
        out_specs=[vmem] * 4,
        scratch_shapes=[
            pltpu.VMEM(queries.shape, BF16),
            pltpu.VMEM(queries.shape, BF16),
            pltpu.VMEM((groups, window, 2 * head_width), BF16),
            pltpu.VMEM((2 * head_width, window), BF16),
            pltpu.VMEM((window, LANES), F32),
            pltpu.VMEM((window, LANES), F32),
            pltpu.VMEM((window, LANES), BF16),
            pltpu.VMEM((window, 2 * head_width), F32),
            pltpu.VMEM((groups, window, 2 * head_width), BF16),
            pltpu.VMEM((groups, reach * tokens, 2 * head_width), BF16),
            dma((2 * groups + 2,)),
            dma((groups, reach)),
            dma((groups, reach)),
            dma((groups, reach)),
            dma((groups, reach)),
        ],
        compiler_params=pltpu.CompilerParams(collective_id=0, has_side_effects=True),
    )(doc_lengths, queries, keys, values, grad_out)
    return attended, grad_queries, grad_keys.astype(BF16), grad_values.astype(BF16)


def solution(mesh):
    rows = P(("ctx", "kvh"), None)
    return jax.shard_map(
        functools.partial(on_device, mesh.shape["ctx"], mesh.shape["kvh"]),
        mesh=mesh,
        in_specs=(rows, rows, rows, rows, P()),
        out_specs=(rows, rows, rows, rows),
        check_vma=False,
    )
```

```python
import functools
import math

import jax
import jax.numpy as jnp
from jax import lax
from jax.experimental import pallas as pl
from jax.experimental.pallas import tpu as pltpu
from jax.sharding import PartitionSpec as P

REACH = 4
LANES = 256
SPAN = 3
NEG_LARGE = -1e30
F32 = jnp.float32
BF16 = jnp.bfloat16
MESH = pl.DeviceIdType.MESH


def matmul(a, b):
    return lax.dot_general(a, b, (((1,), (0,)), ((), ())), preferred_element_type=F32)


def kernel(
    ranges, groups, head_width, doc_ref, q_hbm, k_hbm, v_hbm, do_hbm,
    att_ref, gq_ref, gk_out, gv_out,
    q_ref, do_ref, kv_ref, kvt_ref, bias_ref, s_ref, e_ref, acc_ref, out_ref, in_ref, pair_ref, prior_ref, gk_ref, gv_ref,
    load_sem, kv_send, kv_recv, pass_send, back_send, back_recv, pair_recv,
):
    tokens = q_ref.shape[0]
    reach = REACH * groups
    slots = reach + 1
    window = slots * tokens
    heads = q_ref.shape[1] // head_width // groups
    per_step = LANES // tokens
    spans = [
        pl.ds(a * tokens, min(SPAN, slots - a) * tokens) for a in range(0, slots, SPAN)
    ]
    steps = heads // per_step
    blocks = ranges * groups
    scale = 1.0 / math.sqrt(head_width)
    scale_2 = scale * math.log2(math.e)
    me = lax.axis_index("ctx") * groups + lax.axis_index("kvh")

    place = me % reach
    band = me - place
    core = (place // groups) % 2
    chip = place - core * groups
    toward_partner = groups * (1 - 2 * core)

    def device(block):
        return (block // groups, block % groups)

    def both(*conditions):
        held = conditions[0]
        for condition in conditions[1:]:
            held = jnp.logical_and(held, condition)
        return held

    def core_of(at):
        return (at // groups) % 2

    def chip_of(at):
        return at - core_of(at) * groups

    def shared(source, at):
        first = chip_of(at)
        return both(
            chip_of(source) != first,
            jnp.logical_or(source < first, source > first + groups),
        )

    def reached(d):
        target = (place + d) % reach
        relayed = both(core_of(target) != core, shared(place, target))
        own = place + d < reach
        exists = jnp.logical_or(own, band > 0)
        return target, own, both(exists, jnp.logical_not(relayed))

    def source_of(d):
        source = (place - d + reach) % reach
        exists = me - d >= 0
        pair = both(exists, shared(source, place))
        same = core_of(source) == core
        return source, exists, both(pair, same), both(pair, jnp.logical_not(same))

    def slot(s):
        return pl.ds(s * tokens, tokens)

    own_loads = []
    for g in range(groups):
        columns = pl.ds(g * head_width, head_width)
        for i, src in enumerate((k_hbm, v_hbm)):
            own_loads.append(
                pltpu.make_async_copy(
                    src.at[:, columns],
                    kv_ref.at[g, slot(reach), pl.ds(i * head_width, head_width)],
                    load_sem.at[2 * g + i],
                )
            )
    big_loads = [
        pltpu.make_async_copy(q_hbm, q_ref, load_sem.at[2 * groups]),
        pltpu.make_async_copy(do_hbm, do_ref, load_sem.at[2 * groups + 1]),
    ]
    for copy in own_loads + big_loads:
        copy.start()

    barrier = pltpu.get_barrier_semaphore()
    for d in range(1, reach):
        pl.semaphore_signal(
            barrier, 1, device_id=device(band + (place + d) % reach), device_id_type=MESH
        )
    has_next = me + reach < blocks
    has_prior = band > 0

    @pl.when(has_next)
    def _():
        pl.semaphore_signal(barrier, 1, device_id=device(me + reach), device_id_type=MESH)

    @pl.when(has_prior)
    def _():
        pl.semaphore_signal(barrier, 1, device_id=device(me - reach), device_id_type=MESH)

    def send(src, dst, send_sem, recv_sem, block):
        return pltpu.make_async_remote_copy(
            src_ref=src, dst_ref=dst, send_sem=send_sem, recv_sem=recv_sem,
            device_id=device(block), device_id_type=MESH,
        )

    def kv_copy(g, d, source_slot, block):
        return send(
            kv_ref.at[g, slot(source_slot), :], kv_ref.at[g, slot(reach - d), :],
            kv_send.at[g, d - 1], kv_recv.at[g, d - 1], block,
        )

    def kv_pass(g, d):
        other = d + toward_partner
        return send(
            kv_ref.at[g, slot(reach - d), :],
            kv_ref.at[g, pl.ds(pl.multiple_of((reach - other) * tokens, tokens), tokens), :],
            pass_send.at[g, d - 1], kv_recv.at[g, other - 1], me + toward_partner,
        )

    def back_pair(g, d):
        other = d + toward_partner
        return send(
            out_ref.at[g, slot(reach - d), :],
            pair_ref.at[g, pl.ds(pl.multiple_of((other - 1) * tokens, tokens), tokens), :],
            back_send.at[g, d - 1], pair_recv.at[g, other - 1], me + toward_partner,
        )

    def back_copy(g, d):
        block = me - reach if d == reach else band + (place - d + reach) % reach
        return send(
            out_ref.at[g, slot(reach - d), :], in_ref.at[g, slot(d - 1), :],
            back_send.at[g, d - 1], back_recv.at[g, d - 1], block,
        )

    pl.semaphore_wait(
        barrier, reach - 1 + jnp.where(has_next, 1, 0) + jnp.where(has_prior, 1, 0)
    )
    for copy in own_loads:
        copy.wait()
    for g in range(groups):

        @pl.when(has_next)
        def _():
            kv_copy(g, reach, reach, me + reach).start()

        for d in range(1, reach):
            target, own, straight = reached(d)

            @pl.when(both(own, straight))
            def _():
                kv_copy(g, d, reach, band + target).start()

    def forward_prior(g):
        @pl.when(has_prior)
        def _():
            kv_copy(g, reach, reach, me).wait_recv()

        for d in range(1, reach):
            target, own, straight = reached(d)

            @pl.when(both(jnp.logical_not(own), straight))
            def _():
                kv_copy(g, d, 0, band + target).start()

    def relay(g):
        for d in range(1, reach):
            _, _, relays, _ = source_of(d)

            @pl.when(relays)
            def _():
                kv_copy(g, d, reach, me).wait_recv()
                kv_pass(g, d).start()

    def receive(g):
        for d in range(1, reach):
            _, exists, relays, _ = source_of(d)

            @pl.when(both(exists, jnp.logical_not(relays)))
            def _():
                kv_copy(g, d, reach, me).wait_recv()

    def add_rows(target_ref, g, s, part_ref, rows):
        target_ref[g, slot(s), :] = (
            target_ref[g, slot(s), :].astype(F32) + part_ref[g, rows, :].astype(F32)
        ).astype(BF16)

    def send_partials(g):
        for d in range(1, reach):
            _, exists, relays, relayed = source_of(d)

            @pl.when(relayed)
            def _():
                back_pair(g, d).start()

            @pl.when(both(exists, jnp.logical_not(relays), jnp.logical_not(relayed)))
            def _():
                back_copy(g, d).start()

    def send_pair_sums(g):
        for d in range(1, reach):
            _, _, relays, _ = source_of(d)

            @pl.when(relays)
            def _():
                send(
                    out_ref.at[g, slot(reach - d), :], pair_ref.at[g, slot(d - 1), :],
                    back_send.at[g, d - 1], pair_recv.at[g, d - 1], me + toward_partner,
                ).wait_recv()
                add_rows(out_ref, g, reach - d, pair_ref, slot(d - 1))
                back_copy(g, d).start()

    def send_band_sums(g):
        for d in range(1, reach):
            _, own, straight = reached(d)

            @pl.when(both(jnp.logical_not(own), straight))
            def _():
                back_copy(g, d).wait_recv()
                part = in_ref[g, slot(d - 1), :].astype(F32)
                prior_ref[g] += part

        @pl.when(has_prior)
        def _():
            out_ref[g, slot(0), :] = prior_ref[g].astype(BF16)
            back_copy(g, reach).start()

    def collect(g):
        columns = slice(g * head_width, (g + 1) * head_width)

        def add(d):
            back_copy(g, d).wait_recv()
            part = in_ref[g, slot(d - 1), :].astype(F32)
            gk_ref[:, columns] += part[:, :head_width]
            gv_ref[:, columns] += part[:, head_width:]

        for d in range(1, reach):
            _, own, straight = reached(d)

            @pl.when(both(own, straight))
            def _():
                add(d)

        @pl.when(has_next)
        def _():
            add(reach)

    for d in range(1, reach + 1):

        @pl.when(me - d < 0)
        def _():
            for g in range(groups):
                kv_ref[g, slot(reach - d), :] = jnp.zeros((tokens, 2 * head_width), BF16)

    query_pos = me * tokens + lax.broadcasted_iota(jnp.int32, (8, LANES), 1) % tokens

    def next_doc(i, carry):
        start, first = carry
        first = jnp.where(start <= query_pos, jnp.maximum(first, start), first)
        return start + doc_ref[i], first

    _, doc_first = lax.fori_loop(
        0, doc_ref.shape[0], next_doc, (jnp.int32(0), jnp.zeros((8, LANES), jnp.int32))
    )
    for s in range(slots):
        key_pos = (me - reach + s) * tokens + lax.broadcasted_iota(jnp.int32, (tokens, LANES), 0)
        allowed = (key_pos >= doc_first[0:1]) & (key_pos <= query_pos[0:1])
        bias_ref[slot(s), :] = jnp.where(allowed, 0.0, NEG_LARGE)

    for copy in big_loads:
        copy.wait()

    forward_prior(0)
    relay(0)
    if groups > 1:
        forward_prior(1)

    for g in range(groups):
        receive(g)

        for s in range(slots):
            kvt_ref[:, slot(s)] = kv_ref[g, slot(s), :].T

        acc_ref[...] = jnp.zeros_like(acc_ref)

        def step(i, carry):
            first_head = g * heads + i * per_step

            def head_columns(j):
                return pl.ds(pl.multiple_of((first_head + j) * head_width, head_width), head_width)

            def stacked(ref):
                return jnp.concatenate([ref[:, head_columns(j)] for j in range(per_step)], axis=0)

            q = stacked(q_ref)
            do = stacked(do_ref)
            q_t = q.T
            do_t = do.T
            top = jnp.full((8, LANES), NEG_LARGE, F32)
            for rows in spans:
                scores = matmul(kv_ref[g, rows, :head_width], q_t) * scale_2 + bias_ref[rows, :]
                s_ref[rows, :] = scores
                top = jnp.maximum(top, jnp.max(scores.reshape(-1, 8, LANES), axis=0))
            row_max = jnp.max(top, axis=0, keepdims=True)
            total = jnp.zeros((8, LANES), F32)
            for rows in spans:
                weights = jnp.exp2(s_ref[rows, :] - row_max)
                total = total + jnp.sum(weights.reshape(-1, 8, LANES), axis=0)
                e_ref[rows, :] = weights.astype(BF16)
            inverse = 1.0 / jnp.sum(total, axis=0, keepdims=True)
            out_t = (matmul(kvt_ref[head_width:, :], e_ref[...]) * inverse).astype(BF16)
            delta = jnp.sum(out_t.astype(F32) * do_t.astype(F32), axis=0, keepdims=True)
            out = out_t.T
            scaled_do = (do_t.astype(F32) * inverse).astype(BF16).T
            gq_t = jnp.zeros((head_width, LANES), F32)
            for rows in spans:
                weights = e_ref[rows, :]
                grad_probs = matmul(kv_ref[g, rows, head_width:], do_t)
                grad_scores = (weights.astype(F32) * ((grad_probs - delta) * inverse)).astype(BF16)
                gq_t = gq_t + matmul(kvt_ref[:head_width, rows], grad_scores)
                acc_ref[rows, :head_width] += matmul(grad_scores, q)
                acc_ref[rows, head_width:] += matmul(weights, scaled_do)
            gq = (gq_t * scale).astype(BF16).T
            for j in range(per_step):
                att_ref[:, head_columns(j)] = out[j * tokens:(j + 1) * tokens]
                gq_ref[:, head_columns(j)] = gq[j * tokens:(j + 1) * tokens]
            return carry

        lax.fori_loop(0, steps - 1, step, 0)
        if g + 1 < groups:
            relay(g + 1)
        if g + 2 < groups:
            forward_prior(g + 2)
        if g > 0:
            send_pair_sums(g - 1)
        lax.fori_loop(steps - 1, steps, step, 0)
        if g > 0:
            send_band_sums(g - 1)

        for d in range(1, reach):
            out_ref[g, slot(reach - d), :head_width] = (
                acc_ref[slot(reach - d), :head_width] * scale
            ).astype(BF16)
            out_ref[g, slot(reach - d), head_width:] = acc_ref[slot(reach - d), head_width:].astype(BF16)
        send_partials(g)
        prior_ref[g, :, :head_width] = acc_ref[slot(0), :head_width] * scale
        prior_ref[g, :, head_width:] = acc_ref[slot(0), head_width:]
        columns = slice(g * head_width, (g + 1) * head_width)
        gk_ref[:, columns] = acc_ref[slot(reach), :head_width] * scale
        gv_ref[:, columns] = acc_ref[slot(reach), head_width:]

    send_pair_sums(groups - 1)
    send_band_sums(groups - 1)
    for g in range(groups):
        collect(g)
    gk_out[...] = gk_ref[...].astype(BF16)
    gv_out[...] = gv_ref[...].astype(BF16)

    for g in range(groups):

        @pl.when(has_next)
        def _():
            kv_copy(g, reach, reach, me).wait_send()

        @pl.when(has_prior)
        def _():
            back_copy(g, reach).wait_send()

        for d in range(1, reach):
            _, _, straight = reached(d)
            _, exists, relays, _ = source_of(d)

            @pl.when(straight)
            def _():
                kv_copy(g, d, reach, me).wait_send()

            @pl.when(relays)
            def _():
                kv_pass(g, d).wait_send()

            @pl.when(exists)
            def _():
                back_copy(g, d).wait_send()


def on_device(ranges, groups, queries, keys, values, grad_out, doc_lengths):
    tokens = queries.shape[0]
    head_width = keys.shape[1] // groups
    reach = REACH * groups
    window = (reach + 1) * tokens
    anywhere = pl.BlockSpec(memory_space=pl.ANY)
    vmem = pl.BlockSpec(memory_space=pltpu.VMEM)
    dma = pltpu.SemaphoreType.DMA
    attended, grad_queries, grad_keys, grad_values = pl.pallas_call(
        functools.partial(kernel, ranges, groups, head_width),
        out_shape=(
            jax.ShapeDtypeStruct(queries.shape, BF16),
            jax.ShapeDtypeStruct(queries.shape, BF16),
            jax.ShapeDtypeStruct(keys.shape, BF16),
            jax.ShapeDtypeStruct(keys.shape, BF16),
        ),
        in_specs=[pl.BlockSpec(memory_space=pltpu.SMEM)] + [anywhere] * 4,
        out_specs=[vmem] * 4,
        scratch_shapes=[
            pltpu.VMEM(queries.shape, BF16),
            pltpu.VMEM(queries.shape, BF16),
            pltpu.VMEM((groups, window, 2 * head_width), BF16),
            pltpu.VMEM((2 * head_width, window), BF16),
            pltpu.VMEM((window, LANES), F32),
            pltpu.VMEM((window, LANES), F32),
            pltpu.VMEM((window, LANES), BF16),
            pltpu.VMEM((window, 2 * head_width), F32),
            pltpu.VMEM((groups, window, 2 * head_width), BF16),
            pltpu.VMEM((groups, reach * tokens, 2 * head_width), BF16),
            pltpu.VMEM((groups, reach * tokens, 2 * head_width), BF16),
            pltpu.VMEM((groups, tokens, 2 * head_width), F32),
            pltpu.VMEM(keys.shape, F32),
            pltpu.VMEM(keys.shape, F32),
            dma((2 * groups + 2,)),
            dma((groups, reach)),
            dma((groups, reach)),
            dma((groups, reach)),
            dma((groups, reach)),
            dma((groups, reach)),
            dma((groups, reach)),
        ],
        compiler_params=pltpu.CompilerParams(collective_id=0, has_side_effects=True),
    )(doc_lengths, queries, keys, values, grad_out)
    return attended, grad_queries, grad_keys, grad_values


def solution(mesh):
    rows = P(("ctx", "kvh"), None)
    return jax.shard_map(
        functools.partial(on_device, mesh.shape["ctx"], mesh.shape["kvh"]),
        mesh=mesh,
        in_specs=(rows, rows, rows, rows, P()),
        out_specs=(rows, rows, rows, rows),
        check_vma=False,
    )
```

```python
import functools
import math

import jax
import jax.numpy as jnp
from jax import lax
from jax.experimental import pallas as pl
from jax.experimental.pallas import tpu as pltpu
from jax.sharding import PartitionSpec as P

REACH = 4
LANES = 256
SPAN = 3
NEG_LARGE = -1e30
F32 = jnp.float32
BF16 = jnp.bfloat16
MESH = pl.DeviceIdType.MESH


def matmul(a, b):
    return lax.dot_general(a, b, (((1,), (0,)), ((), ())), preferred_element_type=F32)


def kernel(
    ranges, groups, head_width, doc_ref, q_hbm, k_hbm, v_hbm, do_hbm,
    att_ref, gq_ref, gk_out, gv_out,
    q_ref, do_ref, kv_ref, kvt_ref, bias_ref, s_bufs, e_bufs, acc_ref, out_ref, in_ref, pair_ref, prior_ref, gk_ref, gv_ref,
    load_sem, kv_send, kv_recv, pass_send, back_send, back_recv, pair_recv,
):
    tokens = q_ref.shape[0]
    reach = REACH * groups
    slots = reach + 1
    window = slots * tokens
    heads = q_ref.shape[1] // head_width // groups
    per_step = LANES // tokens
    spans = [
        pl.ds(a * tokens, min(SPAN, slots - a) * tokens) for a in range(0, slots, SPAN)
    ]
    steps = heads // per_step
    blocks = ranges * groups
    scale = 1.0 / math.sqrt(head_width)
    scale_2 = scale * math.log2(math.e)
    me = lax.axis_index("ctx") * groups + lax.axis_index("kvh")

    place = me % reach
    band = me - place
    core = (place // groups) % 2
    chip = place - core * groups
    toward_partner = groups * (1 - 2 * core)

    def device(block):
        return (block // groups, block % groups)

    def both(*conditions):
        held = conditions[0]
        for condition in conditions[1:]:
            held = jnp.logical_and(held, condition)
        return held

    def core_of(at):
        return (at // groups) % 2

    def chip_of(at):
        return at - core_of(at) * groups

    def shared(source, at):
        first = chip_of(at)
        return both(
            chip_of(source) != first,
            jnp.logical_or(source < first, source > first + groups),
        )

    def reached(d):
        target = (place + d) % reach
        relayed = both(core_of(target) != core, shared(place, target))
        own = place + d < reach
        exists = jnp.logical_or(own, band > 0)
        return target, own, both(exists, jnp.logical_not(relayed))

    def source_of(d):
        source = (place - d + reach) % reach
        exists = me - d >= 0
        pair = both(exists, shared(source, place))
        same = core_of(source) == core
        return source, exists, both(pair, same), both(pair, jnp.logical_not(same))

    def slot(s):
        return pl.ds(s * tokens, tokens)

    own_loads = []
    for g in range(groups):
        columns = pl.ds(g * head_width, head_width)
        for i, src in enumerate((k_hbm, v_hbm)):
            own_loads.append(
                pltpu.make_async_copy(
                    src.at[:, columns],
                    kv_ref.at[g, slot(reach), pl.ds(i * head_width, head_width)],
                    load_sem.at[2 * g + i],
                )
            )
    big_loads = [
        pltpu.make_async_copy(q_hbm, q_ref, load_sem.at[2 * groups]),
        pltpu.make_async_copy(do_hbm, do_ref, load_sem.at[2 * groups + 1]),
    ]
    for copy in own_loads + big_loads:
        copy.start()

    barrier = pltpu.get_barrier_semaphore()
    for d in range(1, reach):
        pl.semaphore_signal(
            barrier, 1, device_id=device(band + (place + d) % reach), device_id_type=MESH
        )
    has_next = me + reach < blocks
    has_prior = band > 0

    @pl.when(has_next)
    def _():
        pl.semaphore_signal(barrier, 1, device_id=device(me + reach), device_id_type=MESH)

    @pl.when(has_prior)
    def _():
        pl.semaphore_signal(barrier, 1, device_id=device(me - reach), device_id_type=MESH)

    def send(src, dst, send_sem, recv_sem, block):
        return pltpu.make_async_remote_copy(
            src_ref=src, dst_ref=dst, send_sem=send_sem, recv_sem=recv_sem,
            device_id=device(block), device_id_type=MESH,
        )

    def kv_copy(g, d, source_slot, block):
        return send(
            kv_ref.at[g, slot(source_slot), :], kv_ref.at[g, slot(reach - d), :],
            kv_send.at[g, d - 1], kv_recv.at[g, d - 1], block,
        )

    def kv_pass(g, d):
        other = d + toward_partner
        return send(
            kv_ref.at[g, slot(reach - d), :],
            kv_ref.at[g, pl.ds(pl.multiple_of((reach - other) * tokens, tokens), tokens), :],
            pass_send.at[g, d - 1], kv_recv.at[g, other - 1], me + toward_partner,
        )

    def back_pair(g, d):
        other = d + toward_partner
        return send(
            out_ref.at[g, slot(reach - d), :],
            pair_ref.at[g, pl.ds(pl.multiple_of((other - 1) * tokens, tokens), tokens), :],
            back_send.at[g, d - 1], pair_recv.at[g, other - 1], me + toward_partner,
        )

    def back_copy(g, d):
        block = me - reach if d == reach else band + (place - d + reach) % reach
        return send(
            out_ref.at[g, slot(reach - d), :], in_ref.at[g, slot(d - 1), :],
            back_send.at[g, d - 1], back_recv.at[g, d - 1], block,
        )

    pl.semaphore_wait(
        barrier, reach - 1 + jnp.where(has_next, 1, 0) + jnp.where(has_prior, 1, 0)
    )
    for copy in own_loads:
        copy.wait()
    for g in range(groups):

        @pl.when(has_next)
        def _():
            kv_copy(g, reach, reach, me + reach).start()

        for d in range(1, reach):
            target, own, straight = reached(d)

            @pl.when(both(own, straight))
            def _():
                kv_copy(g, d, reach, band + target).start()

    def forward_prior(g):
        @pl.when(has_prior)
        def _():
            kv_copy(g, reach, reach, me).wait_recv()

        for d in range(1, reach):
            target, own, straight = reached(d)

            @pl.when(both(jnp.logical_not(own), straight))
            def _():
                kv_copy(g, d, 0, band + target).start()

    def relay(g):
        for d in range(1, reach):
            _, _, relays, _ = source_of(d)

            @pl.when(relays)
            def _():
                kv_copy(g, d, reach, me).wait_recv()
                kv_pass(g, d).start()

    def receive(g):
        for d in range(1, reach):
            _, exists, relays, _ = source_of(d)

            @pl.when(both(exists, jnp.logical_not(relays)))
            def _():
                kv_copy(g, d, reach, me).wait_recv()

    def add_rows(target_ref, g, s, part_ref, rows):
        target_ref[g, slot(s), :] = (
            target_ref[g, slot(s), :].astype(F32) + part_ref[g, rows, :].astype(F32)
        ).astype(BF16)

    def send_partials(g):
        for d in range(1, reach):
            _, exists, relays, relayed = source_of(d)

            @pl.when(relayed)
            def _():
                back_pair(g, d).start()

            @pl.when(both(exists, jnp.logical_not(relays), jnp.logical_not(relayed)))
            def _():
                back_copy(g, d).start()

    def send_pair_sums(g):
        for d in range(1, reach):
            _, _, relays, _ = source_of(d)

            @pl.when(relays)
            def _():
                send(
                    out_ref.at[g, slot(reach - d), :], pair_ref.at[g, slot(d - 1), :],
                    back_send.at[g, d - 1], pair_recv.at[g, d - 1], me + toward_partner,
                ).wait_recv()
                add_rows(out_ref, g, reach - d, pair_ref, slot(d - 1))
                back_copy(g, d).start()

    def send_band_sums(g):
        for d in range(1, reach):
            _, own, straight = reached(d)

            @pl.when(both(jnp.logical_not(own), straight))
            def _():
                back_copy(g, d).wait_recv()
                part = in_ref[g, slot(d - 1), :].astype(F32)
                prior_ref[g] += part

        @pl.when(has_prior)
        def _():
            out_ref[g, slot(0), :] = prior_ref[g].astype(BF16)
            back_copy(g, reach).start()

    def collect(g):
        columns = slice(g * head_width, (g + 1) * head_width)

        def add(d):
            back_copy(g, d).wait_recv()
            part = in_ref[g, slot(d - 1), :].astype(F32)
            gk_ref[:, columns] += part[:, :head_width]
            gv_ref[:, columns] += part[:, head_width:]

        for d in range(1, reach):
            _, own, straight = reached(d)

            @pl.when(both(own, straight))
            def _():
                add(d)

        @pl.when(has_next)
        def _():
            add(reach)

    for d in range(1, reach + 1):

        @pl.when(me - d < 0)
        def _():
            for g in range(groups):
                kv_ref[g, slot(reach - d), :] = jnp.zeros((tokens, 2 * head_width), BF16)

    query_pos = me * tokens + lax.broadcasted_iota(jnp.int32, (8, LANES), 1) % tokens

    def next_doc(i, carry):
        start, first = carry
        first = jnp.where(start <= query_pos, jnp.maximum(first, start), first)
        return start + doc_ref[i], first

    _, doc_first = lax.fori_loop(
        0, doc_ref.shape[0], next_doc, (jnp.int32(0), jnp.zeros((8, LANES), jnp.int32))
    )
    for s in range(slots):
        key_pos = (me - reach + s) * tokens + lax.broadcasted_iota(jnp.int32, (tokens, LANES), 0)
        allowed = (key_pos >= doc_first[0:1]) & (key_pos <= query_pos[0:1])
        bias_ref[slot(s), :] = jnp.where(allowed, 0.0, NEG_LARGE)

    for copy in big_loads:
        copy.wait()

    forward_prior(0)
    relay(0)
    if groups > 1:
        forward_prior(1)

    for g in range(groups):
        receive(g)

        for s in range(slots):
            kvt_ref[:, slot(s)] = kv_ref[g, slot(s), :].T

        acc_ref[...] = jnp.zeros_like(acc_ref)

        def step(i, carry, s_ref, e_ref):
            first_head = g * heads + i * per_step

            def head_columns(j):
                return pl.ds((first_head + j) * head_width, head_width)

            def stacked(ref):
                return jnp.concatenate([ref[:, head_columns(j)] for j in range(per_step)], axis=0)

            q = stacked(q_ref)
            do = stacked(do_ref)
            q_t = q.T
            do_t = do.T
            top = jnp.full((8, LANES), NEG_LARGE, F32)
            for rows in spans:
                scores = matmul(kv_ref[g, rows, :head_width], q_t) * scale_2 + bias_ref[rows, :]
                s_ref[rows, :] = scores
                top = jnp.maximum(top, jnp.max(scores.reshape(-1, 8, LANES), axis=0))
            row_max = jnp.max(top, axis=0, keepdims=True)
            total = jnp.zeros((8, LANES), F32)
            for rows in spans:
                weights = jnp.exp2(s_ref[rows, :] - row_max)
                total = total + jnp.sum(weights.reshape(-1, 8, LANES), axis=0)
                e_ref[rows, :] = weights.astype(BF16)
            inverse = 1.0 / jnp.sum(total, axis=0, keepdims=True)
            out_t = (matmul(kvt_ref[head_width:, :], e_ref[...]) * inverse).astype(BF16)
            delta = jnp.sum(out_t.astype(F32) * do_t.astype(F32), axis=0, keepdims=True)
            out = out_t.T
            scaled_do = (do_t.astype(F32) * inverse).astype(BF16).T
            gq_t = jnp.zeros((head_width, LANES), F32)
            for rows in spans:
                weights = e_ref[rows, :]
                grad_probs = matmul(kv_ref[g, rows, head_width:], do_t)
                grad_scores = (weights.astype(F32) * ((grad_probs - delta) * inverse)).astype(BF16)
                gq_t = gq_t + matmul(kvt_ref[:head_width, rows], grad_scores)
                acc_ref[rows, :head_width] += matmul(grad_scores, q)
                acc_ref[rows, head_width:] += matmul(weights, scaled_do)
            gq = (gq_t * scale).astype(BF16).T
            for j in range(per_step):
                att_ref[:, head_columns(j)] = out[j * tokens:(j + 1) * tokens]
                gq_ref[:, head_columns(j)] = gq[j * tokens:(j + 1) * tokens]
            return carry

        for i in range(steps - 1):
            step(i, 0, s_bufs.at[i % 2], e_bufs.at[i % 2])
        if g + 1 < groups:
            relay(g + 1)
        if g + 2 < groups:
            forward_prior(g + 2)
        if g > 0:
            send_pair_sums(g - 1)
        step(steps - 1, 0, s_bufs.at[0], e_bufs.at[0])
        if g > 0:
            send_band_sums(g - 1)

        for d in range(1, reach):
            out_ref[g, slot(reach - d), :head_width] = (
                acc_ref[slot(reach - d), :head_width] * scale
            ).astype(BF16)
            out_ref[g, slot(reach - d), head_width:] = acc_ref[slot(reach - d), head_width:].astype(BF16)
        send_partials(g)
        prior_ref[g, :, :head_width] = acc_ref[slot(0), :head_width] * scale
        prior_ref[g, :, head_width:] = acc_ref[slot(0), head_width:]
        columns = slice(g * head_width, (g + 1) * head_width)
        gk_ref[:, columns] = acc_ref[slot(reach), :head_width] * scale
        gv_ref[:, columns] = acc_ref[slot(reach), head_width:]

    send_pair_sums(groups - 1)
    send_band_sums(groups - 1)
    for g in range(groups):
        collect(g)
    gk_out[...] = gk_ref[...].astype(BF16)
    gv_out[...] = gv_ref[...].astype(BF16)

    for g in range(groups):

        @pl.when(has_next)
        def _():
            kv_copy(g, reach, reach, me).wait_send()

        @pl.when(has_prior)
        def _():
            back_copy(g, reach).wait_send()

        for d in range(1, reach):
            _, _, straight = reached(d)
            _, exists, relays, _ = source_of(d)

            @pl.when(straight)
            def _():
                kv_copy(g, d, reach, me).wait_send()

            @pl.when(relays)
            def _():
                kv_pass(g, d).wait_send()

            @pl.when(exists)
            def _():
                back_copy(g, d).wait_send()


def on_device(ranges, groups, queries, keys, values, grad_out, doc_lengths):
    tokens = queries.shape[0]
    head_width = keys.shape[1] // groups
    reach = REACH * groups
    window = (reach + 1) * tokens
    anywhere = pl.BlockSpec(memory_space=pl.ANY)
    vmem = pl.BlockSpec(memory_space=pltpu.VMEM)
    dma = pltpu.SemaphoreType.DMA
    attended, grad_queries, grad_keys, grad_values = pl.pallas_call(
        functools.partial(kernel, ranges, groups, head_width),
        out_shape=(
            jax.ShapeDtypeStruct(queries.shape, BF16),
            jax.ShapeDtypeStruct(queries.shape, BF16),
            jax.ShapeDtypeStruct(keys.shape, BF16),
            jax.ShapeDtypeStruct(keys.shape, BF16),
        ),
        in_specs=[pl.BlockSpec(memory_space=pltpu.SMEM)] + [anywhere] * 4,
        out_specs=[vmem] * 4,
        scratch_shapes=[
            pltpu.VMEM(queries.shape, BF16),
            pltpu.VMEM(queries.shape, BF16),
            pltpu.VMEM((groups, window, 2 * head_width), BF16),
            pltpu.VMEM((2 * head_width, window), BF16),
            pltpu.VMEM((window, LANES), F32),
            pltpu.VMEM((2, window, LANES), F32),
            pltpu.VMEM((2, window, LANES), BF16),
            pltpu.VMEM((window, 2 * head_width), F32),
            pltpu.VMEM((groups, window, 2 * head_width), BF16),
            pltpu.VMEM((groups, reach * tokens, 2 * head_width), BF16),
            pltpu.VMEM((groups, reach * tokens, 2 * head_width), BF16),
            pltpu.VMEM((groups, tokens, 2 * head_width), F32),
            pltpu.VMEM(keys.shape, F32),
            pltpu.VMEM(keys.shape, F32),
            dma((2 * groups + 2,)),
            dma((groups, reach)),
            dma((groups, reach)),
            dma((groups, reach)),
            dma((groups, reach)),
            dma((groups, reach)),
            dma((groups, reach)),
        ],
        compiler_params=pltpu.CompilerParams(collective_id=0, has_side_effects=True),
    )(doc_lengths, queries, keys, values, grad_out)
    return attended, grad_queries, grad_keys, grad_values


def solution(mesh):
    rows = P(("ctx", "kvh"), None)
    return jax.shard_map(
        functools.partial(on_device, mesh.shape["ctx"], mesh.shape["kvh"]),
        mesh=mesh,
        in_specs=(rows, rows, rows, rows, P()),
        out_specs=(rows, rows, rows, rows),
        check_vma=False,
    )
```
